32 devices in a mesh: replica: 4 (over z), expert: 4 (over y, core), fsdp: 2 (over x).
Axes of the slice: x: 2, y: 2, z: 4, core: 2. Of those that a mesh axis runs over, the one named last changes fastest.
Arguments:
- tokens: bfloat16 [2048, 4096], P(('replica', 'expert'), 'fsdp'), may hold values from -6 to 6
- expert_ids: int32 [2048, 2], P(('replica', 'expert')), may hold values from 0 to 3, all different within a row; in each aligned block of 128 rows (0 to 127, 128 to 255, ...) at most 80 rows name the same one
- router: float32 [4, 4096], P('expert'), may hold values from -5 to 5
- router_moment: float32 [4, 4096], P('expert'), may hold values from -3 to 3
- router_grads: float32 [4, 4, 4096], P('replica', 'expert'), may hold values from -3 to 3
- kv_weight: float32 [4096, 1024], P('expert', 'fsdp'), may hold values from -5 to 5
- kv_moment: float32 [4096, 1024], P('expert', 'fsdp'), may hold values from -3 to 3
- kv_grads: float32 [4, 4096, 1024], P('replica', 'expert', 'fsdp'), may hold values from -3 to 3
- w_gate: bfloat16 [4, 4096, 1024], P('expert', None, 'fsdp'), may hold values from -0.09375 to 0.09375
- w_up: bfloat16 [4, 4096, 1024], P('expert', None, 'fsdp'), may hold values from -0.09375 to 0.09375
- w_down: bfloat16 [4, 1024, 4096], P('expert', 'fsdp'), may hold values from -0.1875 to 0.1875
Outputs:
- mixture: bfloat16 [2048, 4096], P(('replica', 'expert'), 'fsdp')
- router_next: float32 [4, 4096], P('expert')
- router_moment_next: float32 [4, 4096], P('expert')
- kv_next: float32 [4096, 1024], P('expert', 'fsdp')
- kv_moment_next: float32 [4096, 1024], P('expert', 'fsdp')
The draws below stay inside these ranges and needn't reach their ends.
Inputs may be any that keep to these rules, and one draw needn't show every extreme that they name: `expert_ids`: each row names 2 different experts. Within the rows of one replica and expert index (aligned blocks of 128 rows) no expert is named more than 80 times, a bound that some block reaches.
All inputs are finite; a program needn't handle non-finite values.
Results may differ from the reference program's by a relative error of at most 0.015.
Values may be sent and summed in bfloat16 or wider, within the bound.
A program may use at most 64 MiB of HBM per device.

```python
import math
import jax
import jax.numpy as jnp
import numpy as np
from jax import lax

D = 4096
HID = 1024
KV = 1024
TOPK = 2
TOK_DEV = 128
CAP = 80
EXPERTS = 4
REPLICAS = 4
TOKENS = 2048


def steps_of(rng, extent, shards, smallest, top_value):
    loudness, own = 1.0, jax.random.fold_in(rng, 6)
    for dim, shards_of in shards:
        heights = jnp.exp(jax.random.uniform(jax.random.fold_in(own, dim), (shards_of,), jnp.float32, smallest / len(shards), top_value / len(shards)))
        loudness = loudness * jnp.repeat(heights, extent[dim] // shards_of).reshape([-1 if axis == dim else 1 for axis in range(len(extent))])
    return loudness


def deal_out(stream_key, own, number, rows, count, top, reach, slope):
    ranking = jax.random.permutation(stream_key, count)
    packed, common = load_shares(count, rows * top, reach, slope, True), load_shares(count, rows * top, reach, slope, False)
    places = jnp.arange(count)

    def named(lengths, offset_by):
        used = int((lengths > 0).sum())
        fixed = max(1, used // 4)
        moved = fixed + (places - fixed + offset_by * (used - fixed)) % max(1, count - fixed)
        return jnp.zeros((count,), jnp.int32).at[ranking[jnp.where(places < fixed, places, moved)]].set(jnp.asarray(lengths, jnp.int32))

    lengths = jnp.where(number % 4 == 0, named(packed, number // 4), named(common, number - number // 4 - 1))
    mixed = jax.random.permutation(jax.random.fold_in(own, 3), count)
    source_of, sink = mixed[0:count // 2 * 2:2], mixed[1:count // 2 * 2:2]
    margin = jnp.minimum(lengths[source_of] - 1, reach - lengths[sink]) // 2
    margin = jnp.where((source_of == ranking[0]) | (sink == ranking[0]) | (lengths[sink] == 0), 0, jnp.maximum(margin, 0))
    moved = jax.random.randint(jax.random.fold_in(own, 4), (count // 2,), 0, 1 << 20) % (margin + 1)
    lengths = lengths.at[source_of].add(-moved).at[sink].add(moved)
    items = jnp.searchsorted(jnp.cumsum(lengths), jnp.arange(rows * top), side="right").astype(jnp.int32)
    listing = items.reshape(top, rows).T
    listing = listing[jax.random.permutation(jax.random.fold_in(own, 1), rows)]
    offset_by = jax.random.randint(jax.random.fold_in(own, 2), (rows, 1), 0, top)
    return jnp.take_along_axis(listing, (jnp.arange(top)[None, :] + offset_by) % top, axis=1)


def load_shares(number_of, total, limit, slope, full):
    portions = [(1 << 20) // math.isqrt(rank ** slope) + 1 for rank in range(1, number_of + 1)]
    largest = limit if full else min(limit, max(-(-total // number_of), total * portions[0] // sum(portions)))
    least = 1 if total - largest >= number_of - 1 else 0
    given, rest = [largest] + [least] * (number_of - 1), total - largest - least * (number_of - 1)
    while rest > 0:
        movable = [i for i in range(1, number_of) if given[i] < largest] or [i for i in range(1, number_of) if given[i] < limit]
        pool, left = sum([portions[i] for i in movable]), rest
        for i in movable:
            more = min(limit - given[i], max(1, left * portions[i] // pool), rest)
            given[i] = given[i] + more
            rest = rest - more
    return np.array(given)


def normal_values(stream_key, dims, spread, reach, pieces=(), kind=jnp.bfloat16):
    drawn = jax.random.normal(stream_key, dims, jnp.float32) * spread
    if len(pieces) > 0:
        drawn = steps_of(stream_key, dims, pieces, -0.22, 0.18) * drawn
    return jnp.clip(drawn, min=-reach, max=reach).astype(kind)


def setup_inputs(seed: int = 0) -> dict:
    splits = jax.random.split(jax.random.key(seed), 12)
    tokens = normal_values(splits[0], (TOKENS, D), 1.0, 6.0, ((0, 16), (1, 2)))
    expert_ids_keys = jax.random.split(jax.random.fold_in(splits[1], 1), TOKENS // TOK_DEV)
    expert_ids_turns = jax.random.permutation(jax.random.fold_in(splits[1], 3), TOKENS // TOK_DEV)
    expert_ids = jax.vmap(lambda own, number: deal_out(jax.random.fold_in(splits[1], 2), own, number, TOK_DEV, EXPERTS, TOPK, CAP, 2))(expert_ids_keys, expert_ids_turns).reshape((TOKENS, TOPK))
    router = normal_values(splits[2], (EXPERTS, D), 1.0, 5.0, ((0, 4),), jnp.float32)
    router_moment = normal_values(splits[3], (EXPERTS, D), 0.5, 3.0, ((0, 4),), jnp.float32)
    router_grads = normal_values(splits[4], (REPLICAS, EXPERTS, D), 0.5, 3.0, ((0, 4), (1, 4)), jnp.float32)
    kv_weight = normal_values(splits[5], (D, KV), 1.0, 5.0, ((0, 4), (1, 2)), jnp.float32)
    kv_moment = normal_values(splits[6], (D, KV), 0.5, 3.0, ((0, 4), (1, 2)), jnp.float32)
    kv_grads = normal_values(splits[7], (REPLICAS, D, KV), 0.5, 3.0, ((0, 4), (1, 4), (2, 2)), jnp.float32)
    w_gate = normal_values(splits[8], (EXPERTS, D, HID), D ** -0.5, 0.09375, ((0, 4), (2, 2)))
    w_up = normal_values(splits[9], (EXPERTS, D, HID), D ** -0.5, 0.09375, ((0, 4), (2, 2)))
    w_down = normal_values(splits[10], (EXPERTS, HID, D), HID ** -0.5, 0.1875, ((0, 4), (1, 2)))
    return {"tokens": tokens, "expert_ids": expert_ids, "router": router, "router_moment": router_moment, "router_grads": router_grads, "kv_weight": kv_weight, "kv_moment": kv_moment, "kv_grads": kv_grads, "w_gate": w_gate, "w_up": w_up, "w_down": w_down}


def outer_update(param, moment, grads):
    mean = lax.optimization_barrier(jnp.sum(grads, axis=0)) / REPLICAS
    moment_next = 0.9 * moment + mean
    return (param - 0.7 * (mean + 0.9 * moment_next), moment_next)

def reference(tokens, expert_ids, router, router_moment, router_grads, kv_weight, kv_moment, kv_grads, w_gate, w_up, w_down):
    router_next, router_moment_next = outer_update(router, router_moment, router_grads)
    kv_next, kv_moment_next = outer_update(kv_weight, kv_moment, kv_grads)
    blocks = TOKENS // TOK_DEV
    grouped = expert_ids.reshape(blocks, TOK_DEV, TOPK)
    columns = jnp.arange(EXPERTS, dtype=jnp.int32)
    onehot = (grouped[:, :, :, None] == columns).astype(jnp.int32)
    named = lax.optimization_barrier(jnp.sum(onehot, axis=2))
    before = jnp.cumsum(named, axis=1) - named
    position = lax.optimization_barrier(jnp.sum(onehot * before[:, :, None, :], axis=3))
    block_ids = jnp.arange(blocks, dtype=jnp.int32)[:, None, None]
    slot = grouped * (blocks * CAP) + block_ids * CAP + position
    owner = jnp.broadcast_to(jnp.arange(TOKENS, dtype=jnp.int32).reshape(blocks, TOK_DEV, 1), slot.shape)
    inverse = jnp.full((EXPERTS * blocks * CAP,), TOKENS, jnp.int32)
    inverse = inverse.at[slot.reshape(-1)].set(owner.reshape(-1))
    padded = jnp.concatenate([tokens, jnp.zeros((1, D), jnp.bfloat16)], axis=0)

    def one_expert(carry, inputs):
        numer, denom = carry
        gate_w, up_w, down_w, router_row, index = inputs
        rows_idx = lax.dynamic_slice_in_dim(inverse, (index * blocks * CAP).astype(jnp.int32), blocks * CAP, 0)
        rows = padded[rows_idx]
        gate = jnp.dot(rows, gate_w, preferred_element_type=jnp.float32)
        up = jnp.dot(rows, up_w, preferred_element_type=jnp.float32)
        hidden = (jax.nn.silu(gate) * up).astype(jnp.bfloat16)
        out = jnp.dot(hidden, down_w, preferred_element_type=jnp.float32)
        logit = jnp.dot(rows.astype(jnp.float32), router_row, precision=lax.Precision.HIGHEST)
        score = jax.nn.sigmoid(logit / math.sqrt(D))
        weighted = (score[:, None] * out).astype(jnp.bfloat16)
        numer = numer.at[rows_idx].add(weighted.astype(jnp.float32))
        denom = denom.at[rows_idx].add(score)
        return ((numer, denom), None)
    init = (jnp.zeros((TOKENS + 1, D), jnp.float32), jnp.zeros((TOKENS + 1,), jnp.float32))
    (numer, denom), _ = lax.scan(one_expert, init, (w_gate, w_up, w_down, router_next, jnp.arange(EXPERTS, dtype=jnp.int32)))
    mixture = (numer[:TOKENS] / denom[:TOKENS, None]).astype(jnp.bfloat16)
    return (mixture, router_next, router_moment_next, kv_next, kv_moment_next)
```

```python
import functools
import math

import jax
import jax.numpy as jnp
from jax import lax
from jax.experimental import pallas as pl
from jax.experimental.pallas import tpu as pltpu
from jax.sharding import PartitionSpec as P

D = 4096
MESH = pl.DeviceIdType.MESH
F32 = jnp.float32
BF16 = jnp.bfloat16

def advance(param, moment, mean):
    moment_next = 0.9 * moment + mean
    return (param - 0.7 * (mean + 0.9 * moment_next), moment_next)


def general(
    tokens,
    expert_ids,
    router,
    router_moment,
    router_grads,
    kv_weight,
    kv_moment,
    kv_grads,
    w_gate,
    w_up,
    w_down,
):
    replicas = lax.axis_size("replica")
    sums = (
        lax.psum(router_grads[0].astype(jnp.bfloat16), "replica").astype(jnp.float32),
        lax.psum(kv_grads[0].astype(jnp.bfloat16), "replica").astype(jnp.float32),
    )
    router_next, router_moment_next = advance(router, router_moment, sums[0] / replicas)
    kv_next, kv_moment_next = advance(kv_weight, kv_moment, sums[1] / replicas)
    experts_here = lax.axis_size("expert")
    local_rows = expert_ids.shape[0]
    choices_per = expert_ids.shape[1]
    capacity = 5 * local_rows * choices_per // (4 * experts_here)
    columns = jnp.arange(experts_here, dtype=jnp.int32)
    onehot = (expert_ids[:, :, None] == columns).astype(jnp.int32)
    named = jnp.sum(onehot, axis=1)
    before = jnp.cumsum(named, axis=0) - named
    position = jnp.sum(onehot * before[:, None, :], axis=2)
    slot_index = expert_ids * capacity + position
    slots_all = jnp.arange(experts_here * capacity, dtype=jnp.int32)
    assign = jnp.sum(
        (slot_index[None, :, :] == slots_all[:, None, None]).astype(jnp.float32), axis=2
    ).astype(jnp.bfloat16)
    router_row = router_next[0]
    gate_w = w_gate[0]
    up_w = w_up[0]
    down_w = w_down[0]
    outgoing = jnp.dot(assign, tokens, preferred_element_type=jnp.float32).astype(jnp.bfloat16)
    outgoing = outgoing.reshape(experts_here, capacity, tokens.shape[1])
    received = lax.all_to_all(outgoing, "expert", split_axis=0, concat_axis=0, tiled=True)
    sources = received.shape[0]
    count = received.shape[1]
    rows = received.reshape(sources * count, received.shape[2])
    piece = lax.all_gather(rows, "fsdp", axis=1, tiled=True)
    gate = jnp.dot(piece, gate_w, preferred_element_type=jnp.float32)
    up = jnp.dot(piece, up_w, preferred_element_type=jnp.float32)
    logit = jnp.dot(piece.astype(jnp.float32), router_row, precision=lax.Precision.HIGHEST)
    gate, up, logit = (gate, up, logit)
    hidden = (jax.nn.silu(gate) * up).astype(jnp.bfloat16)
    partial_value = jnp.dot(hidden, down_w, preferred_element_type=jnp.float32)
    summed = lax.psum_scatter(
        partial_value.astype(jnp.bfloat16), "fsdp", scatter_dimension=1, tiled=True
    ).astype(jnp.float32)
    score = jax.nn.sigmoid(logit / math.sqrt(D))
    weighted = (score[:, None] * summed).astype(jnp.bfloat16)
    back_weighted = lax.all_to_all(
        weighted.reshape(sources, count, weighted.shape[1]),
        "expert",
        split_axis=0,
        concat_axis=0,
        tiled=True,
    )
    back_score = lax.all_to_all(
        score.reshape(sources, count).astype(jnp.bfloat16),
        "expert",
        split_axis=0,
        concat_axis=0,
        tiled=True,
    ).astype(jnp.float32)
    gather_back = assign.T
    numer = jnp.dot(
        gather_back,
        back_weighted.reshape(experts_here * capacity, back_weighted.shape[2]),
        preferred_element_type=jnp.float32,
    )
    denom = jnp.dot(
        gather_back.astype(jnp.float32),
        back_score.reshape(experts_here * capacity),
        precision=lax.Precision.HIGHEST,
    )
    mixture = (numer / denom[:, None]).astype(jnp.bfloat16)
    return (mixture, router_next, router_moment_next, kv_next, kv_moment_next)


def tile_of(extent, want):
    while extent % want:
        want //= 2
    return want


def kernel(
    capacity,
    tokens,
    ids,
    router,
    router_moment,
    router_grads,
    kv_weight,
    kv_moment,
    kv_grads,
    w_gate,
    w_up,
    w_down,
    mixture,
    router_next,
    router_moment_next,
    kv_next,
    kv_moment_next,
    tok,
    idbuf,
    rbuf,
    wg,
    wu,
    wd,
    rows,
    gacc,
    uacc,
    lacc,
    hidden,
    score,
    dsrc,
    dens,
    outp,
    sib,
    xa,
    yb,
    ya2,
    xb2,
    mixed,
    kg,
    kw,
    km,
    kvb,
    kr1,
    kr2,
    kfin,
    ssem,
    rsem,
    lsem,
    osem,
):
    z = lax.axis_index("replica")
    e = lax.axis_index("expert")
    x = lax.axis_index("fsdp")
    half_e = lax.axis_size("expert") // 2
    replicas = lax.axis_size("replica")
    core = e % 2
    e_sib = e + 1 - 2 * core
    e_y = (e + half_e) % (2 * half_e)
    e_diag = e_y + 1 - 2 * core
    sibling = {"expert": e_sib}
    xn = {"fsdp": 1 - x}
    yn = {"expert": e_y}
    diag = {"expert": e_diag}
    z_one = {"replica": z + 1 - 2 * (z % 2)}
    z_two = {"replica": (z + 2) % replicas}
    n_tok, feat = tokens.shape
    upper = n_tok // 2
    hid = wg.shape[1]
    kv_rows = kg.shape[0] // 4
    used = []

    def send(src, dst, number, device):
        copy = pltpu.make_async_remote_copy(
            src_ref=src,
            dst_ref=dst,
            send_sem=ssem.at[number],
            recv_sem=rsem.at[number],
            device_id=device,
            device_id_type=MESH,
        )
        copy.start()
        used.append(copy)

    def arrive(dst, number, device):
        pltpu.make_async_remote_copy(
            src_ref=dst,
            dst_ref=dst,
            send_sem=ssem.at[number],
            recv_sem=rsem.at[number],
            device_id=device,
            device_id_type=MESH,
        ).wait_recv()

    def load(src, dst, number):
        copy = pltpu.make_async_copy(src, dst, lsem.at[number])
        copy.start()
        return copy

    A = pl.ds(0, upper)
    B = pl.ds(upper, upper)

    get_grads = load(kv_grads.at[0], kg, 0)
    get_own = load(tokens, tok.at[0, 1, 0], 1)
    get_ids = load(ids, idbuf.at[0, 1], 2)
    get_router = load(router_grads.at[0], rbuf.at[z], 3)

    barrier = pltpu.get_barrier_semaphore()
    peers = [sibling, xn, yn, diag] + [{"replica": (z + d) % replicas} for d in (1, 2, 3)]
    for peer in peers:
        pl.semaphore_signal(barrier, inc=1, device_id=peer, device_id_type=MESH)
    pl.semaphore_wait(barrier, len(peers))

    send(tokens.at[A], tok.at[0, 1, 1, A], 0, xn)
    send(tokens.at[B], tok.at[1, 1, 0, B], 1, yn)
    send(ids, idbuf.at[0, 0], 2, sibling)
    send(ids, idbuf.at[1, 1], 3, yn)
    send(ids, idbuf.at[1, 0], 4, diag)
    for d in (1, 2, 3):
        send(router_grads.at[0], rbuf.at[z], 4 + d, {"replica": (z + d) % replicas})
    send(tokens.at[B], tok.at[0, 1, 1, B], 8, xn)
    send(tokens.at[A], tok.at[1, 1, 0, A], 9, yn)
    send(tokens, tok.at[0, 0, 0], 10, sibling)

    low, high = z % 2, z // 2

    def quarter(hr, qr):
        index = ((low + hr) % 2) * 2 + (high + qr) % 2
        return pl.multiple_of(index * kv_rows, kv_rows)

    step = tile_of(kv_rows, 32)
    get_grads.wait()
    for hr in (1, 0):
        for qr in (0, 1):
            base = quarter(hr, qr)

            @pl.loop(0, kv_rows // step)
            def _(i):
                at = pl.multiple_of(i * step, step)
                kvb[hr, qr, pl.ds(at, step)] = kg[pl.ds(pl.multiple_of(base + at, step), step)].astype(BF16)

        if hr == 1:
            send(kvb.at[1], kr1, 11, z_one)

    get_gate = load(w_gate.at[0], wg, 4)
    get_up = load(w_up.at[0], wu, 5)
    get_down = load(w_down.at[0], wd, 6)
    get_kw = load(kv_weight, kw, 7)
    get_km = load(kv_moment, km, 8)

    arrive(tok.at[0, 1, 1, A], 0, xn)
    send(tok.at[0, 1, 1, A], tok.at[1, 1, 1, A], 12, yn)
    send(tok.at[0, 1, 1, A], tok.at[0, 0, 1, A], 13, sibling)
    arrive(tok.at[1, 1, 0, B], 1, yn)
    send(tok.at[1, 1, 0, B], tok.at[1, 1, 1, B], 14, xn)
    send(tok.at[1, 1, 0, B], tok.at[1, 0, 0, B], 15, sibling)

    get_router.wait()
    for d in (1, 2, 3):
        source = (z + replicas - d) % replicas
        arrive(rbuf.at[source], 4 + d, {"replica": source})
    total = rbuf[0]
    for r in range(1, replicas):
        total = total + rbuf[r]
    router_new, moment_new = advance(router[...], router_moment[...], total / replicas)
    router_next[...] = router_new
    router_moment_next[...] = moment_new

    get_ids.wait()
    arrive(idbuf.at[0, 0], 2, sibling)
    arrive(idbuf.at[1, 1], 3, yn)
    arrive(idbuf.at[1, 0], 4, diag)
    before = (
        lax.broadcasted_iota(jnp.int32, (n_tok, n_tok), 0)
        < lax.broadcasted_iota(jnp.int32, (n_tok, n_tok), 1)
    ).astype(F32).astype(BF16)

    def pick(g, q):
        named = idbuf[g, q]
        hit = jnp.where(named == e.astype(F32), 1.0, 0.0)
        chosen = jnp.sum(hit, axis=0, keepdims=True)
        wide = jnp.broadcast_to(chosen, (16, n_tok))
        place = jnp.dot(wide.astype(BF16), before, preferred_element_type=F32)[0:1]
        slots = lax.broadcasted_iota(jnp.int32, (capacity, n_tok), 0).astype(F32)
        return jnp.where((slots == place) & (chosen > 0.5), 1.0, 0.0)

    arrive(tok.at[0, 1, 1, B], 8, xn)
    send(tok.at[0, 1, 1, B], tok.at[0, 0, 1, B], 16, sibling)
    arrive(tok.at[1, 1, 0, A], 9, yn)
    send(tok.at[1, 1, 0, A], tok.at[1, 0, 0, A], 17, sibling)

    def fold(dst, one, two):
        @pl.loop(0, one.shape[0] // step)
        def _(i):
            at = pl.ds(pl.multiple_of(i * step, step), step)
            dst[at] = (one[at].astype(F32) + two[at].astype(F32)).astype(BF16)

    arrive(kr1, 11, z_one)
    fold(kvb.at[0, 1], kvb.at[0, 1], kr1.at[1])
    send(kvb.at[0, 1], kr2, 18, z_two)
    fold(kvb.at[0, 0], kvb.at[0, 0], kr1.at[0])

    cols = tile_of(feat, 512)
    per = feat // cols

    def expert_rows(g):
        picks = [pick(g, q) for q in (0, 1)]
        lacc[...] = jnp.zeros_like(lacc)
        gacc[...] = jnp.zeros_like(gacc)
        uacc[...] = jnp.zeros_like(uacc)
        narrow = [p.astype(BF16) for p in picks]
        for xr in (0, 1):
            @pl.loop(0, per)
            def _(n):
                here = pl.ds(pl.multiple_of(n * cols, cols), cols)
                deep = pl.ds(pl.multiple_of(((x + xr) % 2) * feat + n * cols, cols), cols)
                for q in (0, 1):
                    rows[pl.ds(q * capacity, capacity)] = jnp.dot(
                        narrow[q], tok[g, q, xr, :, here], preferred_element_type=F32
                    ).astype(BF16)
                block = rows[...]
                gacc[...] += jnp.dot(block, wg[deep], preferred_element_type=F32)
                uacc[...] += jnp.dot(block, wu[deep], preferred_element_type=F32)
                prod = block.astype(F32) * router_next[:, deep]
                part = prod[:, 0:128]
                for j in range(1, cols // 128):
                    part = part + prod[:, j * 128 : (j + 1) * 128]
                lacc[...] += part

        gate = gacc[...]
        hidden[...] = (gate / (1.0 + jnp.exp(-gate)) * uacc[...]).astype(BF16)
        logit = jnp.sum(lacc[...], axis=1, keepdims=True) / math.sqrt(2 * feat)
        score[...] = jnp.broadcast_to(1.0 / (1.0 + jnp.exp(-logit)), score.shape)
        for q in (0, 1):
            spread = lax.dot_general(
                picks[q],
                score[pl.ds(q * capacity, capacity)],
                (((0,), (0,)), ((), ())),
                precision=lax.Precision.HIGHEST,
                preferred_element_type=F32,
            )
            if (g, q) == (0, 1):
                dens[0] = spread
            else:
                dsrc[g, q] = spread
        if g == 0:
            send(dsrc.at[0, 0], dens.at[1], 19, sibling)
        else:
            send(dsrc.at[1, 1], dens.at[2], 20, yn)
            send(dsrc.at[1, 0], dens.at[3], 21, diag)
        return narrow

    def expert_out(g, narrow, xr):
        @pl.loop(0, per)
        def _(n):
            here = pl.ds(pl.multiple_of(n * cols, cols), cols)
            deep = pl.ds(pl.multiple_of(((x + xr) % 2) * feat + n * cols, cols), cols)
            value = jnp.dot(hidden[...], wd[:, deep], preferred_element_type=F32)
            for q in (0, 1):
                own = slice(q * capacity, (q + 1) * capacity)
                scaled = (value[own] * score[pl.ds(q * capacity, capacity), 0:1]).astype(BF16)
                outp[g, q, xr, :, here] = lax.dot_general(
                    narrow[q], scaled, (((0,), (0,)), ((), ())), preferred_element_type=F32
                ).astype(BF16)

    rstep = tile_of(upper, 16)

    def add_rows(dst, one, two, lo, count):
        @pl.loop(0, count // rstep)
        def _(i):
            at = pl.ds(pl.multiple_of(lo + i * rstep, rstep), rstep)
            dst[at] = (one[at].astype(F32) + two[at].astype(F32)).astype(BF16)

    def add_half(dst, lo, two):
        @pl.loop(0, upper // rstep)
        def _(i):
            at = pl.ds(pl.multiple_of(lo + i * rstep, rstep), rstep)
            there = pl.ds(pl.multiple_of(i * rstep, rstep), rstep)
            dst[at] = (dst[at].astype(F32) + two[there].astype(F32)).astype(BF16)

    get_own.wait()
    arrive(tok.at[0, 0, 0], 10, sibling)
    arrive(tok.at[0, 0, 1, A], 13, sibling)
    arrive(tok.at[0, 0, 1, B], 16, sibling)
    get_gate.wait()
    get_up.wait()
    narrow = expert_rows(0)
    get_down.wait()

    arrive(tok.at[1, 1, 1, A], 12, yn)
    send(tok.at[1, 1, 1, A], tok.at[1, 0, 1, A], 22, sibling)
    arrive(tok.at[1, 1, 1, B], 14, xn)
    send(tok.at[1, 1, 1, B], tok.at[1, 0, 1, B], 23, sibling)

    expert_out(0, narrow, 1)
    send(outp.at[0, 0, 1], sib.at[0, 1], 24, sibling)
    expert_out(0, narrow, 0)
    send(outp.at[0, 0, 0], sib.at[0, 0], 25, sibling)

    arrive(kr2, 18, z_two)
    fold(kfin.at[0, 0], kvb.at[0, 0], kr2)
    send(kfin.at[0, 0], kfin.at[0, 1], 26, z_two)

    arrive(sib.at[0, 1], 24, sibling)
    add_rows(outp.at[0, 1, 1], outp.at[0, 1, 1], sib.at[0, 1], 0, n_tok)
    send(outp.at[0, 1, 1, A], xa.at[0], 27, xn)
    arrive(tok.at[1, 0, 0, B], 15, sibling)
    arrive(tok.at[1, 0, 0, A], 17, sibling)
    arrive(tok.at[1, 0, 1, A], 22, sibling)
    arrive(tok.at[1, 0, 1, B], 23, sibling)
    narrow = expert_rows(1)
    expert_out(1, narrow, 1)
    send(outp.at[1, 0, 1], sib.at[1, 1], 28, sibling)
    expert_out(1, narrow, 0)
    send(outp.at[1, 0, 0], sib.at[1, 0], 29, sibling)
    arrive(sib.at[1, 1], 28, sibling)
    add_rows(outp.at[1, 1, 1], outp.at[1, 1, 1], sib.at[1, 1], 0, n_tok)
    send(outp.at[1, 1, 1, A], xa.at[1], 30, xn)
    send(outp.at[1, 1, 1, B], yb.at[1], 31, yn)
    arrive(sib.at[1, 0], 29, sibling)
    add_rows(outp.at[1, 1, 0], outp.at[1, 1, 0], sib.at[1, 0], 0, n_tok)
    send(outp.at[1, 1, 0, B], yb.at[0], 32, yn)

    arrive(kfin.at[0, 1], 26, z_two)
    send(kfin.at[0], kfin.at[1], 33, z_one)

    arrive(sib.at[0, 0], 25, sibling)
    add_rows(outp.at[0, 1, 0], outp.at[0, 1, 0], sib.at[0, 0], 0, n_tok)

    get_kw.wait()
    get_km.wait()
    outs = []

    def finish(hr):
        for qr in (0, 1):
            base = quarter(hr, qr)

            @pl.loop(0, kv_rows // step)
            def _(i):
                at = pl.multiple_of(i * step, step)
                deep = pl.ds(pl.multiple_of(base + at, step), step)
                mean = kfin[hr, qr, pl.ds(at, step)].astype(F32) / replicas
                value, moment = advance(kw[deep], km[deep], mean)
                kw[deep] = value
                km[deep] = moment

            whole = pl.ds(base, kv_rows)
            for k, (src, dst) in enumerate(((kw, kv_next), (km, kv_moment_next))):
                copy = pltpu.make_async_copy(src.at[whole], dst.at[whole], osem.at[hr * 4 + qr * 2 + k])
                copy.start()
                outs.append(copy)

    arrive(xa.at[1], 30, xn)
    add_half(outp.at[1, 1, 0], 0, xa.at[1])
    send(outp.at[1, 1, 0, A], ya2, 34, yn)
    arrive(yb.at[1], 31, yn)
    add_half(outp.at[0, 1, 1], upper, yb.at[1])
    send(outp.at[0, 1, 1, B], xb2, 35, xn)
    finish(0)

    arrive(xa.at[0], 27, xn)
    arrive(yb.at[0], 32, yn)
    arrive(dens.at[1], 19, sibling)
    arrive(dens.at[2], 20, yn)
    arrive(dens.at[3], 21, diag)
    dens[0] = 1.0 / (dens[0] + dens[1] + dens[2] + dens[3])
    arrive(kfin.at[1], 33, z_one)
    finish(1)

    def close(lo, first, second):
        @pl.loop(0, upper // rstep)
        def _(i):
            at = pl.ds(pl.multiple_of(lo + i * rstep, rstep), rstep)
            there = pl.ds(pl.multiple_of(i * rstep, rstep), rstep)
            value = outp[0, 1, 0, at].astype(F32) + first[there].astype(F32)
            value = value + second[there].astype(F32)
            mixed[at] = (value * dens[0, at, 0:1]).astype(BF16)

    arrive(ya2, 34, yn)
    close(0, xa.at[0], ya2)
    copy = pltpu.make_async_copy(mixed.at[A], mixture.at[A], osem.at[8])
    copy.start()
    outs.append(copy)
    arrive(xb2, 35, xn)
    close(upper, yb.at[0], xb2)
    copy = pltpu.make_async_copy(mixed.at[B], mixture.at[B], osem.at[9])
    copy.start()
    outs.append(copy)
    for copy in used:
        copy.wait_send()
    for copy in outs:
        copy.wait()


def fused(
    tokens,
    expert_ids,
    router,
    router_moment,
    router_grads,
    kv_weight,
    kv_moment,
    kv_grads,
    w_gate,
    w_up,
    w_down,
):
    n_tok, feat = tokens.shape
    choices = expert_ids.shape[1]
    capacity = 5 * n_tok * choices // (4 * lax.axis_size("expert"))
    hid = w_gate.shape[2]
    kv_shape = kv_weight.shape
    part = (kv_shape[0] // 4, kv_shape[1])
    ids = jnp.pad(expert_ids.T.astype(F32), ((0, 8 - choices), (0, 0)), constant_values=-1.0)
    hbm = pl.BlockSpec(memory_space=pl.ANY)
    vmem = pl.BlockSpec(memory_space=pltpu.VMEM)
    half = (n_tok // 2, feat)
    cols = tile_of(feat, 512)
    return pl.pallas_call(
        functools.partial(kernel, capacity),
        out_shape=(
            jax.ShapeDtypeStruct(tokens.shape, BF16),
            jax.ShapeDtypeStruct(router.shape, F32),
            jax.ShapeDtypeStruct(router.shape, F32),
            jax.ShapeDtypeStruct(kv_shape, F32),
            jax.ShapeDtypeStruct(kv_shape, F32),
        ),
        in_specs=[hbm, hbm, vmem, vmem] + [hbm] * 7,
        out_specs=(hbm, vmem, vmem, hbm, hbm),
        scratch_shapes=[
            pltpu.VMEM((2, 2, 2, n_tok, feat), BF16),
            pltpu.VMEM((2, 2, 8, n_tok), F32),
            pltpu.VMEM((lax.axis_size("replica"), 1, router.shape[1]), F32),
            pltpu.VMEM(w_gate.shape[1:], BF16),
            pltpu.VMEM(w_up.shape[1:], BF16),
            pltpu.VMEM(w_down.shape[1:], BF16),
            pltpu.VMEM((2 * capacity, cols), BF16),
            pltpu.VMEM((2 * capacity, hid), F32),
            pltpu.VMEM((2 * capacity, hid), F32),
            pltpu.VMEM((2 * capacity, 128), F32),
            pltpu.VMEM((2 * capacity, hid), BF16),
            pltpu.VMEM((2 * capacity, 128), F32),
            pltpu.VMEM((2, 2, n_tok, 128), F32),
            pltpu.VMEM((4, n_tok, 128), F32),
            pltpu.VMEM((2, 2, 2, n_tok, feat), BF16),
            pltpu.VMEM((2, 2, n_tok, feat), BF16),
            pltpu.VMEM((2,) + half, BF16),
            pltpu.VMEM((2,) + half, BF16),
            pltpu.VMEM(half, BF16),
            pltpu.VMEM(half, BF16),
            pltpu.VMEM((n_tok, feat), BF16),
            pltpu.VMEM(kv_shape, F32),
            pltpu.VMEM(kv_shape, F32),
            pltpu.VMEM(kv_shape, F32),
            pltpu.VMEM((2, 2) + part, BF16),
            pltpu.VMEM((2,) + part, BF16),
            pltpu.VMEM(part, BF16),
            pltpu.VMEM((2, 2) + part, BF16),
            pltpu.SemaphoreType.DMA((36,)),
            pltpu.SemaphoreType.DMA((36,)),
            pltpu.SemaphoreType.DMA((9,)),
            pltpu.SemaphoreType.DMA((10,)),
        ],
        compiler_params=pltpu.CompilerParams(
            collective_id=0, has_side_effects=True, vmem_limit_bytes=56 << 20
        ),
        name="step",
    )(
        tokens,
        ids,
        router,
        router_moment,
        router_grads,
        kv_weight,
        kv_moment,
        kv_grads,
        w_gate,
        w_up,
        w_down,
    )


def solution(mesh):
    placed = (
        P(("replica", "expert"), "fsdp"),
        P(("replica", "expert"), None),
        P("expert", None),
        P("expert", None),
        P("replica", "expert", None),
        P("expert", "fsdp"),
        P("expert", "fsdp"),
        P("replica", "expert", "fsdp"),
        P("expert", None, "fsdp"),
        P("expert", None, "fsdp"),
        P("expert", "fsdp", None),
    )
    square = (
        mesh.shape["replica"] == 4 and mesh.shape["expert"] == 4 and mesh.shape["fsdp"] == 2
    )
    return jax.shard_map(
        fused if square else general,
        mesh=mesh,
        in_specs=placed,
        out_specs=(
            P(("replica", "expert"), "fsdp"),
            P("expert", None),
            P("expert", None),
            P("expert", "fsdp"),
            P("expert", "fsdp"),
        ),
        check_vma=False,
    )
```

```python
import functools
import math

import jax
import jax.numpy as jnp
from jax import lax
from jax.experimental import pallas as pl
from jax.experimental.pallas import tpu as pltpu
from jax.sharding import PartitionSpec as P

D = 4096
MESH = pl.DeviceIdType.MESH
F32 = jnp.float32
BF16 = jnp.bfloat16

def advance(param, moment, mean):
    moment_next = 0.9 * moment + mean
    return (param - 0.7 * (mean + 0.9 * moment_next), moment_next)


def general(
    tokens,
    expert_ids,
    router,
    router_moment,
    router_grads,
    kv_weight,
    kv_moment,
    kv_grads,
    w_gate,
    w_up,
    w_down,
):
    replicas = lax.axis_size("replica")
    sums = (
        lax.psum(router_grads[0].astype(jnp.bfloat16), "replica").astype(jnp.float32),
        lax.psum(kv_grads[0].astype(jnp.bfloat16), "replica").astype(jnp.float32),
    )
    router_next, router_moment_next = advance(router, router_moment, sums[0] / replicas)
    kv_next, kv_moment_next = advance(kv_weight, kv_moment, sums[1] / replicas)
    experts_here = lax.axis_size("expert")
    local_rows = expert_ids.shape[0]
    choices_per = expert_ids.shape[1]
    capacity = 5 * local_rows * choices_per // (4 * experts_here)
    columns = jnp.arange(experts_here, dtype=jnp.int32)
    onehot = (expert_ids[:, :, None] == columns).astype(jnp.int32)
    named = jnp.sum(onehot, axis=1)
    before = jnp.cumsum(named, axis=0) - named
    position = jnp.sum(onehot * before[:, None, :], axis=2)
    slot_index = expert_ids * capacity + position
    slots_all = jnp.arange(experts_here * capacity, dtype=jnp.int32)
    assign = jnp.sum(
        (slot_index[None, :, :] == slots_all[:, None, None]).astype(jnp.float32), axis=2
    ).astype(jnp.bfloat16)
    router_row = router_next[0]
    gate_w = w_gate[0]
    up_w = w_up[0]
    down_w = w_down[0]
    outgoing = jnp.dot(assign, tokens, preferred_element_type=jnp.float32).astype(jnp.bfloat16)
    outgoing = outgoing.reshape(experts_here, capacity, tokens.shape[1])
    received = lax.all_to_all(outgoing, "expert", split_axis=0, concat_axis=0, tiled=True)
    sources = received.shape[0]
    count = received.shape[1]
    rows = received.reshape(sources * count, received.shape[2])
    piece = lax.all_gather(rows, "fsdp", axis=1, tiled=True)
    gate = jnp.dot(piece, gate_w, preferred_element_type=jnp.float32)
    up = jnp.dot(piece, up_w, preferred_element_type=jnp.float32)
    logit = jnp.dot(piece.astype(jnp.float32), router_row, precision=lax.Precision.HIGHEST)
    gate, up, logit = (gate, up, logit)
    hidden = (jax.nn.silu(gate) * up).astype(jnp.bfloat16)
    partial_value = jnp.dot(hidden, down_w, preferred_element_type=jnp.float32)
    summed = lax.psum_scatter(
        partial_value.astype(jnp.bfloat16), "fsdp", scatter_dimension=1, tiled=True
    ).astype(jnp.float32)
    score = jax.nn.sigmoid(logit / math.sqrt(D))
    weighted = (score[:, None] * summed).astype(jnp.bfloat16)
    back_weighted = lax.all_to_all(
        weighted.reshape(sources, count, weighted.shape[1]),
        "expert",
        split_axis=0,
        concat_axis=0,
        tiled=True,
    )
    back_score = lax.all_to_all(
        score.reshape(sources, count).astype(jnp.bfloat16),
        "expert",
        split_axis=0,
        concat_axis=0,
        tiled=True,
    ).astype(jnp.float32)
    gather_back = assign.T
    numer = jnp.dot(
        gather_back,
        back_weighted.reshape(experts_here * capacity, back_weighted.shape[2]),
        preferred_element_type=jnp.float32,
    )
    denom = jnp.dot(
        gather_back.astype(jnp.float32),
        back_score.reshape(experts_here * capacity),
        precision=lax.Precision.HIGHEST,
    )
    mixture = (numer / denom[:, None]).astype(jnp.bfloat16)
    return (mixture, router_next, router_moment_next, kv_next, kv_moment_next)


def tile_of(extent, want):
    while extent % want:
        want //= 2
    return want


def kernel(
    capacity,
    tokens,
    ids,
    router,
    router_moment,
    router_grads,
    kv_weight,
    kv_moment,
    kv_grads,
    w_gate,
    w_up,
    w_down,
    mixed,
    router_next,
    router_moment_next,
    kw,
    km,
    tok,
    idbuf,
    rbuf,
    wg,
    wu,
    wd,
    rows,
    gacc,
    uacc,
    lacc,
    hidden,
    score,
    dsrc,
    dens,
    outp,
    sib,
    xa,
    yb,
    ya2,
    xb2,
    kg,
    kvb,
    kr,
    kfin,
    ssem,
    rsem,
    lsem,
):
    z = lax.axis_index("replica")
    e = lax.axis_index("expert")
    x = lax.axis_index("fsdp")
    half_e = lax.axis_size("expert") // 2
    replicas = lax.axis_size("replica")
    core = e % 2
    e_sib = e + 1 - 2 * core
    e_y = (e + half_e) % (2 * half_e)
    e_diag = e_y + 1 - 2 * core
    sibling = {"expert": e_sib}
    xn = {"fsdp": 1 - x}
    yn = {"expert": e_y}
    diag = {"expert": e_diag}
    z_ids = ((z + 2) % replicas, replicas - 1 - z, z + 1 - 2 * (z % 2))
    z_to = [{"replica": other} for other in z_ids]
    n_tok, feat = tokens.shape
    upper = n_tok // 2
    hid = wg.shape[1]
    used = []

    def send(src, dst, number, device):
        copy = pltpu.make_async_remote_copy(
            src_ref=src,
            dst_ref=dst,
            send_sem=ssem.at[number],
            recv_sem=rsem.at[number],
            device_id=device,
            device_id_type=MESH,
        )
        copy.start()
        used.append(copy)

    def arrive(dst, number, device):
        pltpu.make_async_remote_copy(
            src_ref=dst,
            dst_ref=dst,
            send_sem=ssem.at[number],
            recv_sem=rsem.at[number],
            device_id=device,
            device_id_type=MESH,
        ).wait_recv()

    def load(src, dst, number):
        copy = pltpu.make_async_copy(src, dst, lsem.at[number])
        copy.start()
        return copy

    A = pl.ds(0, upper)
    B = pl.ds(upper, upper)

    kv_rows = kg.shape[1]
    get_grads = [
        load(kv_grads.at[0, pl.ds(pl.multiple_of(other * kv_rows, kv_rows), kv_rows)], kg.at[k], (0, 2, 9, 10)[k])
        for k, other in enumerate(z_ids + (z,))
    ]
    get_own = load(tokens, tok.at[0, 1, 0], 1)
    get_router = load(router_grads.at[0], rbuf.at[z], 3)

    named = jnp.full((n_tok, 128), -1.0, F32)
    lane = lax.broadcasted_iota(jnp.int32, (n_tok, 128), 1)
    for k in range(ids.shape[1]):
        named = jnp.where(lane == k, ids[:, k : k + 1].astype(F32), named)
    idbuf[0, 1] = named.T[0:8]

    barrier = pltpu.get_barrier_semaphore()
    peers = [sibling, xn, yn, diag] + [{"replica": (z + d) % replicas} for d in (1, 2, 3)]
    for peer in peers:
        pl.semaphore_signal(barrier, inc=1, device_id=peer, device_id_type=MESH)
    pl.semaphore_wait(barrier, len(peers))

    send(tokens.at[A], tok.at[0, 1, 1, A], 0, xn)
    send(tokens.at[B], tok.at[1, 1, 0, B], 1, yn)
    mine = idbuf.at[0, 1]
    send(mine, idbuf.at[0, 0], 2, sibling)
    send(mine, idbuf.at[1, 1], 3, yn)
    send(mine, idbuf.at[1, 0], 4, diag)
    for d in (1, 2, 3):
        send(router_grads.at[0], rbuf.at[z], 4 + d, {"replica": (z + d) % replicas})
    send(tokens.at[B], tok.at[0, 1, 1, B], 8, xn)
    send(tokens.at[A], tok.at[1, 1, 0, A], 9, yn)
    send(tokens, tok.at[0, 0, 0], 10, sibling)

    step = tile_of(kv_rows, 128)

    def quarter(index):
        return pl.multiple_of(index * kv_rows, kv_rows)

    for k, other in enumerate(z_ids + (z,)):
        get_grads[k].wait()
        for i in range(kv_rows // step):
            at = pl.ds(i * step, step)
            kvb[k, at] = kg[k, at].astype(BF16)
        if k < 3:
            send(kvb.at[k], kr.at[k], 11 + 7 * min(k, 1) + 8 * (k == 2), z_to[k])

    get_gate = load(w_gate.at[0], wg, 4)
    get_up = load(w_up.at[0], wu, 5)
    get_down = load(w_down.at[0], wd, 6)
    get_kw = load(kv_weight, kw, 7)
    get_km = load(kv_moment, km, 8)

    def relay_first():
        arrive(tok.at[0, 1, 1, A], 0, xn)
        send(tok.at[0, 1, 1, A], tok.at[1, 1, 1, A], 12, yn)
        send(tok.at[0, 1, 1, A], tok.at[0, 0, 1, A], 13, sibling)
        arrive(tok.at[1, 1, 0, B], 1, yn)
        send(tok.at[1, 1, 0, B], tok.at[1, 1, 1, B], 14, xn)
        send(tok.at[1, 1, 0, B], tok.at[1, 0, 0, B], 15, sibling)

    def relay_second():
        arrive(tok.at[0, 1, 1, B], 8, xn)
        send(tok.at[0, 1, 1, B], tok.at[0, 0, 1, B], 16, sibling)
        arrive(tok.at[1, 1, 0, A], 9, yn)
        send(tok.at[1, 1, 0, A], tok.at[1, 0, 0, A], 17, sibling)

    get_router.wait()
    for d in (1, 2, 3):
        source = (z + replicas - d) % replicas
        arrive(rbuf.at[source], 4 + d, {"replica": source})
    total = rbuf[0]
    for r in range(1, replicas):
        total = total + rbuf[r]
    router_new, moment_new = advance(router[...], router_moment[...], total / replicas)
    router_next[...] = router_new
    router_moment_next[...] = moment_new

    arrive(idbuf.at[0, 0], 2, sibling)
    arrive(idbuf.at[1, 1], 3, yn)
    arrive(idbuf.at[1, 0], 4, diag)
    before = (
        lax.broadcasted_iota(jnp.int32, (n_tok, n_tok), 0)
        < lax.broadcasted_iota(jnp.int32, (n_tok, n_tok), 1)
    ).astype(F32).astype(BF16)

    def pick(g, q):
        named = idbuf[g, q]
        hit = jnp.where(named == e.astype(F32), 1.0, 0.0)
        chosen = jnp.sum(hit, axis=0, keepdims=True)
        wide = jnp.broadcast_to(chosen, (16, n_tok))
        place = jnp.dot(wide.astype(BF16), before, preferred_element_type=F32)[0:1]
        slots = lax.broadcasted_iota(jnp.int32, (capacity, n_tok), 0).astype(F32)
        return jnp.where((slots == place) & (chosen > 0.5), 1.0, 0.0)

    def sum_quarter():
        for k in range(3):
            arrive(kr.at[k], (11, 18, 26)[k], z_to[k])
        for i in range(kv_rows // step):
            at = pl.ds(i * step, step)
            near = kvb[3, at].astype(F32) + kr[2, at].astype(F32)
            far = kr[0, at].astype(F32) + kr[1, at].astype(F32)
            kfin[3, at] = (near + far).astype(BF16)
        for k in range(3):
            send(kfin.at[3], kfin.at[k], (33, 36, 37)[k], z_to[k])

    cols = tile_of(feat, 512)
    per = feat // cols

    picks, narrow = {}, {}

    def expert_rows(g, xr):
        if xr == 0:
            picks[g] = [pick(g, q) for q in (0, 1)]
            narrow[g] = [p.astype(BF16) for p in picks[g]]
            lacc[g] = jnp.zeros(lacc.shape[1:], F32)
            gacc[g] = jnp.zeros(gacc.shape[1:], F32)
            uacc[g] = jnp.zeros(uacc.shape[1:], F32)

        @pl.loop(0, per)
        def _(n):
            here = pl.ds(pl.multiple_of(n * cols, cols), cols)
            deep = pl.ds(pl.multiple_of(((x + xr) % 2) * feat + n * cols, cols), cols)
            for q in (0, 1):
                rows[pl.ds(q * capacity, capacity)] = jnp.dot(
                    narrow[g][q], tok[g, q, xr, :, here], preferred_element_type=F32
                ).astype(BF16)
            block = rows[...]
            gacc[g] += jnp.dot(block, wg[deep], preferred_element_type=F32)
            uacc[g] += jnp.dot(block, wu[deep], preferred_element_type=F32)
            prod = block.astype(F32) * router_next[:, deep]
            part = prod[:, 0:128]
            for j in range(1, cols // 128):
                part = part + prod[:, j * 128 : (j + 1) * 128]
            lacc[g] += part

    def expert_hidden(g):
        gate = gacc[g]
        hidden[...] = (gate / (1.0 + jnp.exp(-gate)) * uacc[g]).astype(BF16)
        logit = jnp.sum(lacc[g], axis=1, keepdims=True) / math.sqrt(2 * feat)
        score[g] = jnp.broadcast_to(1.0 / (1.0 + jnp.exp(-logit)), score.shape[1:])
        for q in (0, 1):
            spread = lax.dot_general(
                picks[g][q],
                score[g, pl.ds(q * capacity, capacity)],
                (((0,), (0,)), ((), ())),
                precision=lax.Precision.HIGHEST,
                preferred_element_type=F32,
            )
            if (g, q) == (0, 1):
                dens[0] = spread
            else:
                dsrc[g, q] = spread
        if g == 0:
            send(dsrc.at[0, 0], dens.at[1], 19, sibling)
        else:
            send(dsrc.at[1, 1], dens.at[2], 20, yn)
            send(dsrc.at[1, 0], dens.at[3], 21, diag)

    def expert_out(g, xr):
        @pl.loop(0, per)
        def _(n):
            here = pl.ds(pl.multiple_of(n * cols, cols), cols)
            deep = pl.ds(pl.multiple_of(((x + xr) % 2) * feat + n * cols, cols), cols)
            value = jnp.dot(hidden[...], wd[:, deep], preferred_element_type=F32)
            for q in (0, 1):
                own = slice(q * capacity, (q + 1) * capacity)
                scaled = (value[own] * score[g, pl.ds(q * capacity, capacity), 0:1]).astype(BF16)
                outp[g, q, xr, :, here] = lax.dot_general(
                    narrow[g][q], scaled, (((0,), (0,)), ((), ())), preferred_element_type=F32
                ).astype(BF16)

    rstep = tile_of(upper, 32)

    def add_rows(dst, one, two, lo, count):
        @pl.loop(0, count // rstep)
        def _(i):
            at = pl.ds(pl.multiple_of(lo + i * rstep, rstep), rstep)
            dst[at] = one[at] + two[at]

    def add_half(dst, lo, two):
        @pl.loop(0, upper // rstep)
        def _(i):
            at = pl.ds(pl.multiple_of(lo + i * rstep, rstep), rstep)
            there = pl.ds(pl.multiple_of(i * rstep, rstep), rstep)
            dst[at] = dst[at] + two[there]

    def diagonals():
        arrive(tok.at[1, 1, 1, A], 12, yn)
        send(tok.at[1, 1, 1, A], tok.at[1, 0, 1, A], 22, sibling)
        arrive(tok.at[1, 1, 1, B], 14, xn)
        send(tok.at[1, 1, 1, B], tok.at[1, 0, 1, B], 23, sibling)

    get_gate.wait()
    get_up.wait()
    get_own.wait()
    arrive(tok.at[0, 0, 0], 10, sibling)
    expert_rows(0, 0)
    relay_first()
    relay_second()
    arrive(tok.at[0, 0, 1, A], 13, sibling)
    arrive(tok.at[0, 0, 1, B], 16, sibling)
    expert_rows(0, 1)
    expert_hidden(0)
    get_down.wait()
    expert_out(0, 1)
    send(outp.at[0, 0, 1], sib.at[0, 1], 24, sibling)
    arrive(tok.at[1, 0, 0, B], 15, sibling)
    arrive(tok.at[1, 0, 0, A], 17, sibling)
    expert_rows(1, 0)
    diagonals()
    arrive(sib.at[0, 1], 24, sibling)
    add_rows(outp.at[0, 1, 1], outp.at[0, 1, 1], sib.at[0, 1], 0, n_tok)
    send(outp.at[0, 1, 1, A], xa.at[0], 27, xn)
    arrive(tok.at[1, 0, 1, A], 22, sibling)
    arrive(tok.at[1, 0, 1, B], 23, sibling)
    expert_rows(1, 1)
    expert_out(0, 0)
    send(outp.at[0, 0, 0], sib.at[0, 0], 25, sibling)
    expert_hidden(1)
    expert_out(1, 1)
    send(outp.at[1, 0, 1], sib.at[1, 1], 28, sibling)
    expert_out(1, 0)
    send(outp.at[1, 0, 0], sib.at[1, 0], 29, sibling)
    arrive(sib.at[1, 1], 28, sibling)
    add_rows(outp.at[1, 1, 1], outp.at[1, 1, 1], sib.at[1, 1], 0, n_tok)
    send(outp.at[1, 1, 1, A], xa.at[1], 30, xn)
    send(outp.at[1, 1, 1, B], yb.at[1], 31, yn)
    arrive(sib.at[1, 0], 29, sibling)
    add_rows(outp.at[1, 1, 0], outp.at[1, 1, 0], sib.at[1, 0], 0, n_tok)
    send(outp.at[1, 1, 0, B], yb.at[0], 32, yn)

    sum_quarter()

    arrive(sib.at[0, 0], 25, sibling)
    add_rows(outp.at[0, 1, 0], outp.at[0, 1, 0], sib.at[0, 0], 0, n_tok)

    get_kw.wait()
    get_km.wait()

    def finish(k):
        base = quarter((z_ids + (z,))[k])
        for i in range(kv_rows // step):
            deep = pl.ds(pl.multiple_of(base + i * step, step), step)
            mean = kfin[k, pl.ds(i * step, step)].astype(F32) / replicas
            value, moment = advance(kw[deep], km[deep], mean)
            kw[deep] = value
            km[deep] = moment

    arrive(xa.at[1], 30, xn)
    add_half(outp.at[1, 1, 0], 0, xa.at[1])
    send(outp.at[1, 1, 0, A], ya2, 34, yn)
    arrive(yb.at[1], 31, yn)
    add_half(outp.at[0, 1, 1], upper, yb.at[1])
    send(outp.at[0, 1, 1, B], xb2, 35, xn)
    finish(3)

    arrive(xa.at[0], 27, xn)
    arrive(yb.at[0], 32, yn)
    arrive(dens.at[1], 19, sibling)
    arrive(dens.at[2], 20, yn)
    arrive(dens.at[3], 21, diag)
    dens[0] = 1.0 / (dens[0] + dens[1] + dens[2] + dens[3])

    def close(lo, first, second):
        @pl.loop(0, upper // rstep)
        def _(i):
            at = pl.ds(pl.multiple_of(lo + i * rstep, rstep), rstep)
            there = pl.ds(pl.multiple_of(i * rstep, rstep), rstep)
            value = outp[0, 1, 0, at].astype(F32) + first[there].astype(F32)
            value = value + second[there].astype(F32)
            mixed[at] = (value * dens[0, at, 0:1]).astype(BF16)

    arrive(ya2, 34, yn)
    close(0, xa.at[0], ya2)
    arrive(xb2, 35, xn)
    close(upper, yb.at[0], xb2)
    for k in (2, 0, 1):
        arrive(kfin.at[k], (33, 36, 37)[k], z_to[k])
        finish(k)
    for copy in used:
        copy.wait_send()


def fused(
    tokens,
    expert_ids,
    router,
    router_moment,
    router_grads,
    kv_weight,
    kv_moment,
    kv_grads,
    w_gate,
    w_up,
    w_down,
):
    n_tok, feat = tokens.shape
    choices = expert_ids.shape[1]
    capacity = 5 * n_tok * choices // (4 * lax.axis_size("expert"))
    hid = w_gate.shape[2]
    kv_shape = kv_weight.shape
    part = (kv_shape[0] // 4, kv_shape[1])
    hbm = pl.BlockSpec(memory_space=pltpu.HBM)
    vmem = pl.BlockSpec(memory_space=pltpu.VMEM)
    half = (n_tok // 2, feat)
    cols = tile_of(feat, 512)
    outs = (
        jax.ShapeDtypeStruct(tokens.shape, BF16),
        jax.ShapeDtypeStruct(router.shape, F32),
        jax.ShapeDtypeStruct(router.shape, F32),
        jax.ShapeDtypeStruct(kv_shape, F32),
        jax.ShapeDtypeStruct(kv_shape, F32),
    )
    held = pl.pallas_call(
        functools.partial(kernel, capacity),
        out_shape=tuple(pltpu.VMEM(o.shape, o.dtype) for o in outs),
        in_specs=[hbm, vmem, vmem, vmem] + [hbm] * 7,
        out_specs=(vmem,) * 5,
        scratch_shapes=[
            pltpu.VMEM((2, 2, 2, n_tok, feat), BF16),
            pltpu.VMEM((2, 2, 8, n_tok), F32),
            pltpu.VMEM((lax.axis_size("replica"), 1, router.shape[1]), F32),
            pltpu.VMEM(w_gate.shape[1:], BF16),
            pltpu.VMEM(w_up.shape[1:], BF16),
            pltpu.VMEM(w_down.shape[1:], BF16),
            pltpu.VMEM((2 * capacity, cols), BF16),
            pltpu.VMEM((2, 2 * capacity, hid), F32),
            pltpu.VMEM((2, 2 * capacity, hid), F32),
            pltpu.VMEM((2, 2 * capacity, 128), F32),
            pltpu.VMEM((2 * capacity, hid), BF16),
            pltpu.VMEM((2, 2 * capacity, 128), F32),
            pltpu.VMEM((2, 2, n_tok, 128), F32),
            pltpu.VMEM((4, n_tok, 128), F32),
            pltpu.VMEM((2, 2, 2, n_tok, feat), BF16),
            pltpu.VMEM((2, 2, n_tok, feat), BF16),
            pltpu.VMEM((2,) + half, BF16),
            pltpu.VMEM((2,) + half, BF16),
            pltpu.VMEM(half, BF16),
            pltpu.VMEM(half, BF16),
            pltpu.VMEM((4,) + part, F32),
            pltpu.VMEM((4,) + part, BF16),
            pltpu.VMEM((3,) + part, BF16),
            pltpu.VMEM((4,) + part, BF16),
            pltpu.SemaphoreType.DMA((38,)),
            pltpu.SemaphoreType.DMA((38,)),
            pltpu.SemaphoreType.DMA((11,)),
        ],
        compiler_params=pltpu.CompilerParams(
            collective_id=0, has_side_effects=True, vmem_limit_bytes=48 << 20
        ),
        name="step",
    )(
        tokens,
        expert_ids,
        router,
        router_moment,
        router_grads,
        kv_weight,
        kv_moment,
        kv_grads,
        w_gate,
        w_up,
        w_down,
    )
    return held


def solution(mesh):
    placed = (
        P(("replica", "expert"), "fsdp"),
        P(("replica", "expert"), None),
        P("expert", None),
        P("expert", None),
        P("replica", "expert", None),
        P("expert", "fsdp"),
        P("expert", "fsdp"),
        P("replica", "expert", "fsdp"),
        P("expert", None, "fsdp"),
        P("expert", None, "fsdp"),
        P("expert", "fsdp", None),
    )
    square = (
        mesh.shape["replica"] == 4 and mesh.shape["expert"] == 4 and mesh.shape["fsdp"] == 2
    )
    return jax.shard_map(
        fused if square else general,
        mesh=mesh,
        in_specs=placed,
        out_specs=(
            P(("replica", "expert"), "fsdp"),
            P("expert", None),
            P("expert", None),
            P("expert", "fsdp"),
            P("expert", "fsdp"),
        ),
        check_vma=False,
    )
```

```python
import functools
import math

import jax
import jax.numpy as jnp
from jax import lax
from jax.experimental import pallas as pl
from jax.experimental.pallas import tpu as pltpu
from jax.sharding import PartitionSpec as P

D = 4096
MESH = pl.DeviceIdType.MESH
F32 = jnp.float32
BF16 = jnp.bfloat16

def advance(param, moment, mean):
    moment_next = 0.9 * moment + mean
    return (param - 0.7 * (mean + 0.9 * moment_next), moment_next)


def general(
    tokens,
    expert_ids,
    router,
    router_moment,
    router_grads,
    kv_weight,
    kv_moment,
    kv_grads,
    w_gate,
    w_up,
    w_down,
):
    replicas = lax.axis_size("replica")
    sums = (
        lax.psum(router_grads[0].astype(jnp.bfloat16), "replica").astype(jnp.float32),
        lax.psum(kv_grads[0].astype(jnp.bfloat16), "replica").astype(jnp.float32),
    )
    router_next, router_moment_next = advance(router, router_moment, sums[0] / replicas)
    kv_next, kv_moment_next = advance(kv_weight, kv_moment, sums[1] / replicas)
    experts_here = lax.axis_size("expert")
    local_rows = expert_ids.shape[0]
    choices_per = expert_ids.shape[1]
    capacity = 5 * local_rows * choices_per // (4 * experts_here)
    columns = jnp.arange(experts_here, dtype=jnp.int32)
    onehot = (expert_ids[:, :, None] == columns).astype(jnp.int32)
    named = jnp.sum(onehot, axis=1)
    before = jnp.cumsum(named, axis=0) - named
    position = jnp.sum(onehot * before[:, None, :], axis=2)
    slot_index = expert_ids * capacity + position
    slots_all = jnp.arange(experts_here * capacity, dtype=jnp.int32)
    assign = jnp.sum(
        (slot_index[None, :, :] == slots_all[:, None, None]).astype(jnp.float32), axis=2
    ).astype(jnp.bfloat16)
    router_row = router_next[0]
    gate_w = w_gate[0]
    up_w = w_up[0]
    down_w = w_down[0]
    outgoing = jnp.dot(assign, tokens, preferred_element_type=jnp.float32).astype(jnp.bfloat16)
    outgoing = outgoing.reshape(experts_here, capacity, tokens.shape[1])
    received = lax.all_to_all(outgoing, "expert", split_axis=0, concat_axis=0, tiled=True)
    sources = received.shape[0]
    count = received.shape[1]
    rows = received.reshape(sources * count, received.shape[2])
    piece = lax.all_gather(rows, "fsdp", axis=1, tiled=True)
    gate = jnp.dot(piece, gate_w, preferred_element_type=jnp.float32)
    up = jnp.dot(piece, up_w, preferred_element_type=jnp.float32)
    logit = jnp.dot(piece.astype(jnp.float32), router_row, precision=lax.Precision.HIGHEST)
    gate, up, logit = (gate, up, logit)
    hidden = (jax.nn.silu(gate) * up).astype(jnp.bfloat16)
    partial_value = jnp.dot(hidden, down_w, preferred_element_type=jnp.float32)
    summed = lax.psum_scatter(
        partial_value.astype(jnp.bfloat16), "fsdp", scatter_dimension=1, tiled=True
    ).astype(jnp.float32)
    score = jax.nn.sigmoid(logit / math.sqrt(D))
    weighted = (score[:, None] * summed).astype(jnp.bfloat16)
    back_weighted = lax.all_to_all(
        weighted.reshape(sources, count, weighted.shape[1]),
        "expert",
        split_axis=0,
        concat_axis=0,
        tiled=True,
    )
    back_score = lax.all_to_all(
        score.reshape(sources, count).astype(jnp.bfloat16),
        "expert",
        split_axis=0,
        concat_axis=0,
        tiled=True,
    ).astype(jnp.float32)
    gather_back = assign.T
    numer = jnp.dot(
        gather_back,
        back_weighted.reshape(experts_here * capacity, back_weighted.shape[2]),
        preferred_element_type=jnp.float32,
    )
    denom = jnp.dot(
        gather_back.astype(jnp.float32),
        back_score.reshape(experts_here * capacity),
        precision=lax.Precision.HIGHEST,
    )
    mixture = (numer / denom[:, None]).astype(jnp.bfloat16)
    return (mixture, router_next, router_moment_next, kv_next, kv_moment_next)


def tile_of(extent, want):
    while extent % want:
        want //= 2
    return want


def kernel(
    capacity,
    tokens,
    ids,
    router,
    router_moment,
    router_grads,
    kv_weight,
    kv_moment,
    kv_grads,
    w_gate,
    w_up,
    w_down,
    mixed,
    router_next,
    router_moment_next,
    kw,
    km,
    tok,
    idbuf,
    rbuf,
    wg,
    wu,
    wd,
    rows,
    gacc,
    uacc,
    lacc,
    hidden,
    score,
    dsrc,
    dens,
    outp,
    sib,
    xa,
    yb,
    ya2,
    xb2,
    kg,
    kvb,
    kr,
    kfin,
    ssem,
    rsem,
    lsem,
):
    z = lax.axis_index("replica")
    e = lax.axis_index("expert")
    x = lax.axis_index("fsdp")
    half_e = lax.axis_size("expert") // 2
    replicas = lax.axis_size("replica")
    core = e % 2
    e_sib = e + 1 - 2 * core
    e_y = (e + half_e) % (2 * half_e)
    e_diag = e_y + 1 - 2 * core
    sibling = {"expert": e_sib}
    xn = {"fsdp": 1 - x}
    yn = {"expert": e_y}
    diag = {"expert": e_diag}
    z_ids = ((z + 2) % replicas, replicas - 1 - z, z + 1 - 2 * (z % 2))
    z_to = [{"replica": other} for other in z_ids]
    n_tok, feat = tokens.shape
    upper = n_tok // 2
    hid = wg.shape[1]
    used = []

    def send(src, dst, number, device):
        copy = pltpu.make_async_remote_copy(
            src_ref=src,
            dst_ref=dst,
            send_sem=ssem.at[number],
            recv_sem=rsem.at[number],
            device_id=device,
            device_id_type=MESH,
        )
        copy.start()
        used.append(copy)

    def arrive(dst, number, device):
        pltpu.make_async_remote_copy(
            src_ref=dst,
            dst_ref=dst,
            send_sem=ssem.at[number],
            recv_sem=rsem.at[number],
            device_id=device,
            device_id_type=MESH,
        ).wait_recv()

    def load(src, dst, number):
        copy = pltpu.make_async_copy(src, dst, lsem.at[number])
        copy.start()
        return copy

    A = pl.ds(0, upper)
    B = pl.ds(upper, upper)

    kv_rows = kg.shape[1]
    get_grads = [
        load(kv_grads.at[0, pl.ds(pl.multiple_of(other * kv_rows, kv_rows), kv_rows)], kg.at[k], (0, 2, 9, 10)[k])
        for k, other in enumerate(z_ids + (z,))
    ]
    get_own = load(tokens, tok.at[0, 1, 0], 1)
    get_router = load(router_grads.at[0], rbuf.at[z], 3)

    named = jnp.full((n_tok, 128), -1.0, F32)
    lane = lax.broadcasted_iota(jnp.int32, (n_tok, 128), 1)
    for k in range(ids.shape[1]):
        named = jnp.where(lane == k, ids[:, k : k + 1].astype(F32), named)
    idbuf[0, 1] = named.T[0:8]

    barrier = pltpu.get_barrier_semaphore()
    peers = [sibling, xn, yn, diag] + [{"replica": (z + d) % replicas} for d in (1, 2, 3)]
    for peer in peers:
        pl.semaphore_signal(barrier, inc=1, device_id=peer, device_id_type=MESH)
    pl.semaphore_wait(barrier, len(peers))

    send(tokens.at[A], tok.at[0, 1, 1, A], 0, xn)
    send(tokens.at[B], tok.at[1, 1, 0, B], 1, yn)
    mine = idbuf.at[0, 1]
    send(mine, idbuf.at[0, 0], 2, sibling)
    send(mine, idbuf.at[1, 1], 3, yn)
    send(mine, idbuf.at[1, 0], 4, diag)
    for d in (1, 2, 3):
        send(router_grads.at[0], rbuf.at[z], 4 + d, {"replica": (z + d) % replicas})
    send(tokens.at[B], tok.at[0, 1, 1, B], 8, xn)
    send(tokens.at[A], tok.at[1, 1, 0, A], 9, yn)
    send(tokens, tok.at[0, 0, 0], 10, sibling)

    step = tile_of(kv_rows, 128)

    def quarter(index):
        return pl.multiple_of(index * kv_rows, kv_rows)

    for k, other in enumerate(z_ids + (z,)):
        get_grads[k].wait()
        for i in range(kv_rows // step):
            at = pl.ds(i * step, step)
            kvb[k, at] = kg[k, at].astype(BF16)
        if k < 3:
            send(kvb.at[k], kr.at[k], 11 + 7 * min(k, 1) + 8 * (k == 2), z_to[k])

    get_gate = load(w_gate.at[0], wg, 4)
    get_up = load(w_up.at[0], wu, 5)
    get_down = load(w_down.at[0], wd, 6)
    get_kw = load(kv_weight, kw, 7)
    get_km = load(kv_moment, km, 8)

    def relay_first():
        arrive(tok.at[0, 1, 1, A], 0, xn)
        send(tok.at[0, 1, 1, A], tok.at[1, 1, 1, A], 12, yn)
        send(tok.at[0, 1, 1, A], tok.at[0, 0, 1, A], 13, sibling)
        arrive(tok.at[1, 1, 0, B], 1, yn)
        send(tok.at[1, 1, 0, B], tok.at[1, 1, 1, B], 14, xn)
        send(tok.at[1, 1, 0, B], tok.at[1, 0, 0, B], 15, sibling)

    def relay_second():
        arrive(tok.at[0, 1, 1, B], 8, xn)
        send(tok.at[0, 1, 1, B], tok.at[0, 0, 1, B], 16, sibling)
        arrive(tok.at[1, 1, 0, A], 9, yn)
        send(tok.at[1, 1, 0, A], tok.at[1, 0, 0, A], 17, sibling)

    get_router.wait()
    for d in (1, 2, 3):
        source = (z + replicas - d) % replicas
        arrive(rbuf.at[source], 4 + d, {"replica": source})
    total = rbuf[0]
    for r in range(1, replicas):
        total = total + rbuf[r]
    router_new, moment_new = advance(router[...], router_moment[...], total / replicas)
    router_next[...] = router_new
    router_moment_next[...] = moment_new

    arrive(idbuf.at[0, 0], 2, sibling)
    arrive(idbuf.at[1, 1], 3, yn)
    arrive(idbuf.at[1, 0], 4, diag)
    before = (
        lax.broadcasted_iota(jnp.int32, (n_tok, n_tok), 0)
        < lax.broadcasted_iota(jnp.int32, (n_tok, n_tok), 1)
    ).astype(F32).astype(BF16)

    def pick(g, q):
        named = idbuf[g, q]
        hit = jnp.where(named == e.astype(F32), 1.0, 0.0)
        chosen = jnp.sum(hit, axis=0, keepdims=True)
        wide = jnp.broadcast_to(chosen, (16, n_tok))
        place = jnp.dot(wide.astype(BF16), before, preferred_element_type=F32)[0:1]
        slots = lax.broadcasted_iota(jnp.int32, (capacity, n_tok), 0).astype(F32)
        return jnp.where((slots == place) & (chosen > 0.5), 1.0, 0.0)

    def sum_quarter():
        for k in range(3):
            arrive(kr.at[k], (11, 18, 26)[k], z_to[k])
        for i in range(kv_rows // step):
            at = pl.ds(i * step, step)
            near = kvb[3, at].astype(F32) + kr[2, at].astype(F32)
            far = kr[0, at].astype(F32) + kr[1, at].astype(F32)
            kfin[3, at] = (near + far).astype(BF16)
        for k in range(3):
            send(kfin.at[3], kfin.at[k], (33, 36, 37)[k], z_to[k])

    cols = tile_of(feat, 512)
    per = feat // cols

    picks, narrow = {}, {}

    def expert_rows(g, xr):
        if xr == 0:
            picks[g] = [pick(g, q) for q in (0, 1)]
            narrow[g] = [p.astype(BF16) for p in picks[g]]
            lacc[g] = jnp.zeros(lacc.shape[1:], F32)
            gacc[g] = jnp.zeros(gacc.shape[1:], F32)
            uacc[g] = jnp.zeros(uacc.shape[1:], F32)

        @pl.loop(0, per)
        def _(n):
            here = pl.ds(pl.multiple_of(n * cols, cols), cols)
            deep = pl.ds(pl.multiple_of(((x + xr) % 2) * feat + n * cols, cols), cols)
            for q in (0, 1):
                rows[pl.ds(q * capacity, capacity)] = jnp.dot(
                    narrow[g][q], tok[g, q, xr, :, here], preferred_element_type=F32
                ).astype(BF16)
            block = rows[...]
            gacc[g] += jnp.dot(block, wg[deep], preferred_element_type=F32)
            uacc[g] += jnp.dot(block, wu[deep], preferred_element_type=F32)
            prod = block.astype(F32) * router_next[:, deep]
            part = prod[:, 0:128]
            for j in range(1, cols // 128):
                part = part + prod[:, j * 128 : (j + 1) * 128]
            lacc[g] += part

    def expert_hidden(g):
        gate = gacc[g]
        hidden[...] = (gate / (1.0 + jnp.exp(-gate)) * uacc[g]).astype(BF16)
        logit = jnp.sum(lacc[g], axis=1, keepdims=True) / math.sqrt(2 * feat)
        score[g] = jnp.broadcast_to(1.0 / (1.0 + jnp.exp(-logit)), score.shape[1:])
        for q in (0, 1):
            spread = lax.dot_general(
                picks[g][q],
                score[g, pl.ds(q * capacity, capacity)],
                (((0,), (0,)), ((), ())),
                precision=lax.Precision.HIGHEST,
                preferred_element_type=F32,
            )
            if (g, q) == (0, 1):
                dens[0] = spread
            else:
                dsrc[g, q] = spread
        if g == 0:
            send(dsrc.at[0, 0], dens.at[1], 19, sibling)
        else:
            send(dsrc.at[1, 1], dens.at[2], 20, yn)
            send(dsrc.at[1, 0], dens.at[3], 21, diag)

    def expert_out(g, xr):
        @pl.loop(0, per)
        def _(n):
            here = pl.ds(pl.multiple_of(n * cols, cols), cols)
            deep = pl.ds(pl.multiple_of(((x + xr) % 2) * feat + n * cols, cols), cols)
            value = jnp.dot(hidden[...], wd[:, deep], preferred_element_type=F32)
            for q in (0, 1):
                own = slice(q * capacity, (q + 1) * capacity)
                scaled = (value[own] * score[g, pl.ds(q * capacity, capacity), 0:1]).astype(BF16)
                outp[g, q, xr, :, here] = lax.dot_general(
                    narrow[g][q], scaled, (((0,), (0,)), ((), ())), preferred_element_type=F32
                ).astype(BF16)

    rstep = tile_of(upper, 32)

    def add_rows(dst, one, two, lo, count):
        @pl.loop(0, count // rstep)
        def _(i):
            at = pl.ds(pl.multiple_of(lo + i * rstep, rstep), rstep)
            dst[at] = one[at] + two[at]

    def add_half(dst, lo, two):
        @pl.loop(0, upper // rstep)
        def _(i):
            at = pl.ds(pl.multiple_of(lo + i * rstep, rstep), rstep)
            there = pl.ds(pl.multiple_of(i * rstep, rstep), rstep)
            dst[at] = dst[at] + two[there]

    def diagonals():
        arrive(tok.at[1, 1, 1, A], 12, yn)
        send(tok.at[1, 1, 1, A], tok.at[1, 0, 1, A], 22, sibling)
        arrive(tok.at[1, 1, 1, B], 14, xn)
        send(tok.at[1, 1, 1, B], tok.at[1, 0, 1, B], 23, sibling)

    get_gate.wait()
    get_up.wait()
    get_own.wait()
    arrive(tok.at[0, 0, 0], 10, sibling)
    expert_rows(0, 0)
    relay_first()
    relay_second()
    arrive(tok.at[0, 0, 1, A], 13, sibling)
    arrive(tok.at[0, 0, 1, B], 16, sibling)
    expert_rows(0, 1)
    expert_hidden(0)
    get_down.wait()
    expert_out(0, 1)
    send(outp.at[0, 0, 1], sib.at[0, 1], 24, sibling)
    arrive(tok.at[1, 0, 0, B], 15, sibling)
    arrive(tok.at[1, 0, 0, A], 17, sibling)
    expert_rows(1, 0)
    diagonals()
    arrive(sib.at[0, 1], 24, sibling)
    add_rows(outp.at[0, 1, 1], outp.at[0, 1, 1], sib.at[0, 1], 0, n_tok)
    send(outp.at[0, 1, 1, A], xa.at[0], 27, xn)
    arrive(tok.at[1, 0, 1, A], 22, sibling)
    arrive(tok.at[1, 0, 1, B], 23, sibling)
    expert_rows(1, 1)
    expert_out(0, 0)
    send(outp.at[0, 0, 0], sib.at[0, 0], 25, sibling)
    sum_quarter()
    expert_hidden(1)
    expert_out(1, 1)
    send(outp.at[1, 0, 1], sib.at[1, 1], 28, sibling)
    expert_out(1, 0)
    send(outp.at[1, 0, 0], sib.at[1, 0], 29, sibling)
    arrive(sib.at[1, 1], 28, sibling)
    add_rows(outp.at[1, 1, 1], outp.at[1, 1, 1], sib.at[1, 1], 0, n_tok)
    send(outp.at[1, 1, 1, A], xa.at[1], 30, xn)
    send(outp.at[1, 1, 1, B], yb.at[1], 31, yn)
    arrive(sib.at[1, 0], 29, sibling)
    add_rows(outp.at[1, 1, 0], outp.at[1, 1, 0], sib.at[1, 0], 0, n_tok)
    send(outp.at[1, 1, 0, B], yb.at[0], 32, yn)

    arrive(sib.at[0, 0], 25, sibling)
    add_rows(outp.at[0, 1, 0], outp.at[0, 1, 0], sib.at[0, 0], 0, n_tok)

    get_kw.wait()
    get_km.wait()

    def finish(k):
        base = quarter((z_ids + (z,))[k])
        for i in range(kv_rows // step):
            deep = pl.ds(pl.multiple_of(base + i * step, step), step)
            mean = kfin[k, pl.ds(i * step, step)].astype(F32) / replicas
            value, moment = advance(kw[deep], km[deep], mean)
            kw[deep] = value
            km[deep] = moment

    arrive(xa.at[1], 30, xn)
    add_half(outp.at[1, 1, 0], 0, xa.at[1])
    send(outp.at[1, 1, 0, A], ya2, 34, yn)
    arrive(yb.at[1], 31, yn)
    add_half(outp.at[0, 1, 1], upper, yb.at[1])
    send(outp.at[0, 1, 1, B], xb2, 35, xn)
    finish(3)

    arrive(xa.at[0], 27, xn)
    arrive(yb.at[0], 32, yn)
    arrive(dens.at[1], 19, sibling)
    arrive(dens.at[2], 20, yn)
    arrive(dens.at[3], 21, diag)
    dens[0] = 1.0 / (dens[0] + dens[1] + dens[2] + dens[3])

    def close(lo, first, second):
        @pl.loop(0, upper // rstep)
        def _(i):
            at = pl.ds(pl.multiple_of(lo + i * rstep, rstep), rstep)
            there = pl.ds(pl.multiple_of(i * rstep, rstep), rstep)
            value = outp[0, 1, 0, at].astype(F32) + first[there].astype(F32)
            value = value + second[there].astype(F32)
            mixed[at] = (value * dens[0, at, 0:1]).astype(BF16)

    arrive(ya2, 34, yn)
    close(0, xa.at[0], ya2)
    arrive(xb2, 35, xn)
    close(upper, yb.at[0], xb2)
    for k in (2, 0, 1):
        arrive(kfin.at[k], (33, 36, 37)[k], z_to[k])
        finish(k)
    for copy in used:
        copy.wait_send()


def fused(
    tokens,
    expert_ids,
    router,
    router_moment,
    router_grads,
    kv_weight,
    kv_moment,
    kv_grads,
    w_gate,
    w_up,
    w_down,
):
    n_tok, feat = tokens.shape
    choices = expert_ids.shape[1]
    capacity = 5 * n_tok * choices // (4 * lax.axis_size("expert"))
    hid = w_gate.shape[2]
    kv_shape = kv_weight.shape
    part = (kv_shape[0] // 4, kv_shape[1])
    hbm = pl.BlockSpec(memory_space=pltpu.HBM)
    vmem = pl.BlockSpec(memory_space=pltpu.VMEM)
    half = (n_tok // 2, feat)
    cols = tile_of(feat, 512)
    outs = (
        jax.ShapeDtypeStruct(tokens.shape, BF16),
        jax.ShapeDtypeStruct(router.shape, F32),
        jax.ShapeDtypeStruct(router.shape, F32),
        jax.ShapeDtypeStruct(kv_shape, F32),
        jax.ShapeDtypeStruct(kv_shape, F32),
    )
    held = pl.pallas_call(
        functools.partial(kernel, capacity),
        out_shape=tuple(pltpu.VMEM(o.shape, o.dtype) for o in outs),
        in_specs=[hbm, vmem, vmem, vmem] + [hbm] * 7,
        out_specs=(vmem,) * 5,
        scratch_shapes=[
            pltpu.VMEM((2, 2, 2, n_tok, feat), BF16),
            pltpu.VMEM((2, 2, 8, n_tok), F32),
            pltpu.VMEM((lax.axis_size("replica"), 1, router.shape[1]), F32),
            pltpu.VMEM(w_gate.shape[1:], BF16),
            pltpu.VMEM(w_up.shape[1:], BF16),
            pltpu.VMEM(w_down.shape[1:], BF16),
            pltpu.VMEM((2 * capacity, cols), BF16),
            pltpu.VMEM((2, 2 * capacity, hid), F32),
            pltpu.VMEM((2, 2 * capacity, hid), F32),
            pltpu.VMEM((2, 2 * capacity, 128), F32),
            pltpu.VMEM((2 * capacity, hid), BF16),
            pltpu.VMEM((2, 2 * capacity, 128), F32),
            pltpu.VMEM((2, 2, n_tok, 128), F32),
            pltpu.VMEM((4, n_tok, 128), F32),
            pltpu.VMEM((2, 2, 2, n_tok, feat), BF16),
            pltpu.VMEM((2, 2, n_tok, feat), BF16),
            pltpu.VMEM((2,) + half, BF16),
            pltpu.VMEM((2,) + half, BF16),
            pltpu.VMEM(half, BF16),
            pltpu.VMEM(half, BF16),
            pltpu.VMEM((4,) + part, F32),
            pltpu.VMEM((4,) + part, BF16),
            pltpu.VMEM((3,) + part, BF16),
            pltpu.VMEM((4,) + part, BF16),
            pltpu.SemaphoreType.DMA((38,)),
            pltpu.SemaphoreType.DMA((38,)),
            pltpu.SemaphoreType.DMA((11,)),
        ],
        compiler_params=pltpu.CompilerParams(
            collective_id=0, has_side_effects=True, vmem_limit_bytes=59 << 20
        ),
        name="step",
    )(
        tokens,
        expert_ids,
        router,
        router_moment,
        router_grads,
        kv_weight,
        kv_moment,
        kv_grads,
        w_gate,
        w_up,
        w_down,
    )
    return held


def solution(mesh):
    placed = (
        P(("replica", "expert"), "fsdp"),
        P(("replica", "expert"), None),
        P("expert", None),
        P("expert", None),
        P("replica", "expert", None),
        P("expert", "fsdp"),
        P("expert", "fsdp"),
        P("replica", "expert", "fsdp"),
        P("expert", None, "fsdp"),
        P("expert", None, "fsdp"),
        P("expert", "fsdp", None),
    )
    square = (
        mesh.shape["replica"] == 4 and mesh.shape["expert"] == 4 and mesh.shape["fsdp"] == 2
    )
    return jax.shard_map(
        fused if square else general,
        mesh=mesh,
        in_specs=placed,
        out_specs=(
            P(("replica", "expert"), "fsdp"),
            P("expert", None),
            P("expert", None),
            P("expert", "fsdp"),
            P("expert", "fsdp"),
        ),
        check_vma=False,
    )
```
